32 devices in a mesh: parts: 2 (over y), seq: 4 (over z), grp: 2 (over x), sub: 2 (over core).
Axes of the slice: x: 2, y: 2, z: 4, core: 2. Of those that a mesh axis runs over, the one named last changes fastest.
Arguments:
- projected: bfloat16 [2048, 3, 4096], P(('parts', 'seq'), None, ('grp', 'sub')), parts along dimension 0, may hold values from -6 to 6
- short_filter: float32 [3, 3, 4096], P(None, None, ('grp', 'sub')), may hold values from -3.5 to 3.5
- span_lengths: int32 [16], P('parts'), parts along dimension 0, may hold values from 1 to 512, 1024 in all
- mode_rates: float32 [8, 256], P(None, ('grp', 'sub')), may hold values from 4.8828126e-05 to 0.05
- mode_residues: float32 [8, 256], P(None, ('grp', 'sub')), may hold values from -2 to 2
- out_weight: bfloat16 [4096, 4096], P(None, ('grp', 'sub')), may hold values from -0.09375 to 0.09375
Outputs:
- mixed: bfloat16 [2048, 4096], P(('parts', 'seq'), ('grp', 'sub')), parts along dimension 0
The draws below stay inside these ranges and needn't reach their ends.
There are 2 independent parts, one for each index of `parts`. The reference program is written for one: setup_inputs(seed, part) draws one part's arguments, and reference() takes and returns one part's arrays. A program takes and returns all parts, laid end to end along the dimension named above; an argument that names none is the same for every part. Nothing has to cross between parts.
Inputs may be any that keep to these rules, and one draw needn't show every extreme that they name: `span_lengths`: the 8 span lengths, in order, sum to 1024; the longest has exactly 512 tokens.
All inputs are finite; a program needn't handle non-finite values.
Results may differ from the reference program's by a relative error of at most 0.0058.
Values may be sent and summed in bfloat16 or wider, within the bound.
A program may use at most 64 MiB of HBM per device.

```python
import math
import jax
import jax.numpy as jnp
import numpy as np
from jax import lax

D = 4096
SHORT = 3
FG = 256
NMODE = 8
NCHUNK = 8
LENGTH = 1024


def steps_of(own_key, dims, split, least, high):
    factor_of = 1.0
    for position, shards_of in split:
        draws = jax.random.uniform(jax.random.fold_in(jax.random.fold_in(own_key, 6), position), (shards_of,), jnp.float32, least / len(split), high / len(split))
        factor_of = factor_of * jnp.repeat(jnp.exp(draws), dims[position] // shards_of).reshape((-1,) + (1,) * (len(dims) - 1 - position))
    return factor_of


def split_up(number_of, total, reach, lean):
    loads = [(1 << 20) // math.isqrt(grade ** lean) + 1 for grade in range(2, number_of + 1)]
    surplus, counts = total - reach - (number_of - 1), [1] * (number_of - 1)
    while surplus > 0:
        candidates = [i for i in range(number_of - 1) if counts[i] < reach]
        pool, budget = sum([loads[i] for i in candidates]), surplus
        for i in candidates:
            addition = min(reach - counts[i], max(1, budget * loads[i] // pool), surplus)
            counts[i] = counts[i] + addition
            surplus = surplus - addition
    return np.array([reach] + counts)


def ragged_sizes(rng, number_of, total, limit, lean):
    if number_of == 2:
        one = jax.random.randint(rng, (), max(1, total - limit), min(limit, total - 1) + 1)
        return jnp.stack([one, total - one])
    tallies = jnp.asarray(split_up(number_of, total, limit, lean), jnp.int32)
    twos = (number_of - 1) // 2
    giver, sink = tallies[1:1 + 2 * twos:2], tallies[2:2 + 2 * twos:2]
    slack = jnp.minimum(giver - 1, limit - sink)
    moved = jax.random.randint(jax.random.fold_in(rng, 1), (twos,), 0, 1 << 20) % (slack + 1)
    tallies = tallies.at[1:1 + 2 * twos:2].set(giver - moved).at[2:2 + 2 * twos:2].set(sink + moved)
    return tallies[jax.random.permutation(jax.random.fold_in(rng, 2), number_of)]


def bell_draw(rng, extent, width, reach, split=(), held_as=jnp.bfloat16):
    drawn = jax.random.normal(rng, extent, jnp.float32) * width
    if len(split) > 0:
        drawn = steps_of(rng, extent, split, -0.22, 0.18) * drawn
    return jnp.clip(drawn, min=-reach, max=reach).astype(held_as)


def setup_inputs(seed: int = 0, part: int = 0) -> dict:
    key_list = jax.random.split(jax.random.key(seed), 7)
    own_keys = jax.random.split(jax.random.fold_in(key_list[6], part), 7)
    projected = bell_draw(own_keys[0], (LENGTH, 3, D), 1.0, 6.0, ((0, 4), (2, 4)))
    short_filter = bell_draw(key_list[1], (SHORT, 3, D), 3 ** -0.5, 3.5, ((2, 4),), jnp.float32)
    span_lengths = ragged_sizes(own_keys[2], NCHUNK, LENGTH, LENGTH // 2, 2).astype(jnp.int32)
    mode_rates = jnp.clip(jnp.exp(math.log(0.05) - 6.931472 * jax.random.uniform(key_list[3], (NMODE, FG), jnp.float32) ** steps_of(key_list[3], (NMODE, FG), ((1, 4),), -0.2, 0.2)), 4.882812572759576e-05, 0.05)
    mode_residues = bell_draw(key_list[4], (NMODE, FG), 0.35, 2.0, ((1, 4),), jnp.float32)
    out_weight = bell_draw(key_list[5], (D, D), D ** -0.5, 0.09375, ((1, 4),))
    return dict(projected=projected, short_filter=short_filter, span_lengths=span_lengths, mode_rates=mode_rates, mode_residues=mode_residues, out_weight=out_weight)


def span_index(span_lengths, positions):
    span_starts = (jnp.cumsum(span_lengths) - span_lengths).astype(jnp.int32)
    inside = (positions[:, None] >= span_starts[None, :]).astype(jnp.int32)
    return (lax.optimization_barrier(jnp.sum(inside, axis=1)) - 1).astype(jnp.int32)

def reference(projected, short_filter, span_lengths, mode_rates, mode_residues, out_weight):
    positions = jnp.arange(LENGTH, dtype=jnp.int32)
    span_of = span_index(span_lengths, positions)
    source = projected.astype(jnp.float32)
    filtered = short_filter[0][None] * source
    for tap_index in range(1, SHORT):
        shifted = jnp.concatenate([jnp.zeros((tap_index, 3, D), jnp.float32), source[:-tap_index]], axis=0)
        earlier = span_index(span_lengths, (positions - tap_index).astype(jnp.int32))
        same_span = (earlier == span_of).astype(jnp.float32)
        filtered = filtered + short_filter[tap_index][None] * shifted * same_span[:, None, None]
    gated_rows = (filtered[:, 1] * filtered[:, 2]).astype(jnp.bfloat16)
    group_size = D // FG
    decay_mode = jnp.repeat(jnp.exp(-mode_rates), group_size, axis=1)
    mode_weight = jnp.repeat(mode_residues * jnp.sqrt(-jnp.expm1(-2.0 * mode_rates)), group_size, axis=1)
    keep_flag = (span_of == span_index(span_lengths, (positions - 1).astype(jnp.int32))).astype(jnp.float32)

    def advance(carried, inputs):
        gated_row, keep_row = inputs
        carried = decay_mode * carried * keep_row + gated_row[None, :]
        return (carried, lax.optimization_barrier(jnp.sum(mode_weight * carried, axis=0)))
    _, long_out = lax.scan(advance, jnp.zeros((NMODE, D), jnp.float32), (gated_rows.astype(jnp.float32), keep_flag))
    mixed_in = (filtered[:, 0] * long_out).astype(jnp.bfloat16)
    return jnp.dot(mixed_in, out_weight, preferred_element_type=jnp.float32).astype(jnp.bfloat16)
```

```python
import functools

import jax
import jax.numpy as jnp
from jax import lax
from jax.experimental import pallas as pl
from jax.experimental.pallas import tpu as pltpu
from jax.sharding import PartitionSpec as P

MESH = pl.DeviceIdType.MESH
LANES = 128


def kernel(
    sizes, spans_ref, x_ref, taps_ref, modes_ref, weight_hbm, out_ref,
    weight, xq, xk, xv, tap_rows, mode_rows, keep1, keep2, cont,
    halo_out, halo_in, state_out, state_in, incoming, gathered, total,
    weight_sem, halo_send, halo_recv, state_send, state_recv,
    sub_send, sub_recv, grp_send, grp_recv, fwd_send, fwd_recv,
):
    seq, grp, sub, chunk_count = sizes
    _, tokens, channels = x_ref.shape
    modes = modes_ref.shape[0] // 2
    groups = modes_ref.shape[1]
    rows = channels // LANES
    pitch = xq.shape[0] // tokens
    chunk = tokens // chunk_count
    z, g, s = lax.axis_index("seq"), lax.axis_index("grp"), lax.axis_index("sub")
    offset = z * tokens

    barrier = pltpu.get_barrier_semaphore()
    for axis, me, count in (("seq", z, seq), ("grp", g, grp), ("sub", s, sub)):
        for step in range(1, count):
            pl.semaphore_signal(
                barrier, inc=1, device_id={axis: lax.rem(me + step, count)}, device_id_type=MESH
            )
    load_weight = pltpu.make_async_copy(weight_hbm, weight, weight_sem)
    load_weight.start()

    if pitch != rows:
        for buffer in (xq, xk, xv, tap_rows, mode_rows):
            buffer[...] = jnp.zeros_like(buffer)
    for j, buffer in enumerate((xq, xk, xv)):
        for c in range(rows):
            lanes = slice(c * LANES, (c + 1) * LANES)
            buffer[pl.ds(c, tokens, stride=pitch), :] = x_ref[j, :, lanes].astype(jnp.float32)
    tail = 2 * pitch
    for j, buffer in enumerate((xq, xk, xv)):
        halo_out[pl.ds(j * tail, tail), :] = buffer[pl.ds(tokens * pitch - tail, tail), :]
    pl.semaphore_wait(barrier, seq + grp + sub - 3)

    send_halo = pltpu.make_async_remote_copy(
        src_ref=halo_out, dst_ref=halo_in, send_sem=halo_send, recv_sem=halo_recv,
        device_id={"seq": lax.rem(z + 1, seq)}, device_id_type=MESH,
    )

    @pl.when(z < seq - 1)
    def _():
        send_halo.start()

    tap_count = taps_ref.shape[0]
    for k in range(tap_count):
        for c in range(rows):
            for j in range(3):
                tap_rows[pl.ds((k * 3 + j) * pitch + c, 1), :] = taps_ref[
                    k, pl.ds(j, 1), c * LANES : (c + 1) * LANES
                ]
    group_size = channels // groups
    spread = (
        lax.broadcasted_iota(jnp.int32, (groups, channels), 1) // group_size
        == lax.broadcasted_iota(jnp.int32, (groups, channels), 0)
    ).astype(jnp.float32)
    wide = jnp.dot(
        modes_ref[...], spread, precision=lax.Precision.HIGHEST, preferred_element_type=jnp.float32
    )
    for c in range(rows):
        mode_rows[pl.ds(c, 2 * modes, stride=pitch), :] = wide[:, c * LANES : (c + 1) * LANES]

    starts, start = [], jnp.int32(0)
    for i in range(spans_ref.shape[0]):
        starts.append(start)
        start = start + spans_ref[i]
    position = offset + lax.broadcasted_iota(jnp.int32, (tokens, LANES), 0)
    here = position == starts[0]
    before = position - 1 == starts[0]
    cut = (position >= starts[0]) & (starts[0] >= offset)
    for first in starts[1:]:
        here = here | (position == first)
        before = before | (position - 1 == first)
        cut = cut | ((position >= first) & (first >= offset))
    keep1[...] = jnp.where(here, 0.0, 1.0)
    keep2[...] = jnp.where(here | before, 0.0, 1.0)
    cont[...] = jnp.where(cut, 0.0, 1.0)

    def tile(ref, index):
        return ref[pl.ds(pl.multiple_of(index * pitch, pitch), pitch), :]

    rate = [tile(mode_rows, n) for n in range(modes)]
    decay = [jnp.exp(-rate[n]) for n in range(modes)]
    gain = [tile(mode_rows, modes + n) for n in range(modes)]
    taps = [[tile(tap_rows, k * 3 + j) for j in range(3)] for k in range(3)]

    @pl.when(z == 0)
    def _():
        halo_in[...] = jnp.zeros_like(halo_in)

    @pl.when(z > 0)
    def _():
        send_halo.wait_recv()

    unroll = 8

    def scan_block(block, carry):
        last, older, state = carry
        for u in range(unroll):
            t = block * unroll + u
            m1, m2 = keep1[pl.ds(t, 1), :], keep2[pl.ds(t, 1), :]
            now = [tile(buffer, t) for buffer in (xq, xk, xv)]
            filtered = [
                taps[0][j] * now[j] + taps[1][j] * last[j] * m1 + taps[2][j] * older[j] * m2
                for j in range(3)
            ]
            gated = (filtered[1] * filtered[2]).astype(jnp.bfloat16).astype(jnp.float32)
            state = [decay[n] * (state[n] * m1) + gated for n in range(modes)]
            parts = [gain[n] * state[n] for n in range(modes)]
            while len(parts) > 1:
                parts = [sum(parts[i : i + 2][1:], parts[i]) for i in range(0, len(parts), 2)]
            row = pl.ds(pl.multiple_of(t * pitch, pitch), pitch)
            xq[row, :] = filtered[0]
            xk[row, :] = parts[0]
            older, last = last, now
        return last, older, state

    last = [tile(halo_in, 2 * j + 1) for j in range(3)]
    older = [tile(halo_in, 2 * j) for j in range(3)]
    zero = [jnp.zeros((pitch, LANES), jnp.float32)] * modes
    _, _, state = lax.fori_loop(0, tokens // unroll, scan_block, (last, older, zero))
    for n in range(modes):
        state_out[pl.ds(n * pitch, pitch), :] = state[n]

    state_copies = []
    for step in range(1, seq):
        copy = pltpu.make_async_remote_copy(
            src_ref=state_out, dst_ref=state_in.at[step - 1],
            send_sem=state_send.at[step - 1], recv_sem=state_recv.at[step - 1],
            device_id={"seq": lax.rem(z + step, seq)}, device_id_type=MESH,
        )
        state_copies.append(copy)
        pl.when(z + step < seq)(copy.start)
    incoming[...] = jnp.zeros_like(incoming)
    for step in range(1, seq):
        reach = (step - 1) * tokens
        open_ = jnp.float32(1.0)
        for first in starts:
            inside = (first >= offset - reach) & (first <= offset - 1)
            open_ = jnp.where(inside, 0.0, open_)

        @pl.when(z >= step)
        def _():
            state_copies[step - 1].wait_recv()
            for n in range(modes):
                at = pl.ds(n * pitch, pitch)
                factor = gain[n] * jnp.exp(-rate[n] * float(reach)) * open_
                incoming[at, :] += factor * state_in[step - 1, at, :]

    own = g * sub + s
    carried = [tile(incoming, n) for n in range(modes)]

    def correct_block(block, carry):
        for u in range(unroll):
            t = block * unroll + u
            carry = [decay[n] * carry[n] for n in range(modes)]
            parts = carry
            while len(parts) > 1:
                parts = [sum(parts[i : i + 2][1:], parts[i]) for i in range(0, len(parts), 2)]
            row = pl.ds(pl.multiple_of(t * pitch, pitch), pitch)
            xv[row, :] = xq[row, :] * (xk[row, :] + parts[0] * cont[pl.ds(t, 1), :])
        return carry

    def send(slot, c, axis, me, count, step, send_sem, recv_sem):
        piece = gathered.at[slot, pl.ds(c * chunk, chunk), :]
        return pltpu.make_async_remote_copy(
            src_ref=piece, dst_ref=piece, send_sem=send_sem, recv_sem=recv_sem,
            device_id={axis: lax.rem(me + step, count)}, device_id_type=MESH,
        )

    sent = []
    for c in range(chunk_count):
        per = chunk // unroll
        carried = lax.fori_loop(c * per, (c + 1) * per, correct_block, carried)
        for r in range(rows):
            gathered[own, pl.ds(c * chunk, chunk), r * LANES : (r + 1) * LANES] = xv[
                pl.ds(c * chunk * pitch + r, chunk, stride=pitch), :
            ].astype(jnp.bfloat16)
        for step in range(1, grp):
            copy = send(own, c, "grp", g, grp, step, grp_send.at[step - 1, c], grp_recv.at[step - 1, c])
            copy.start()
            sent.append(copy)
        for step in range(1, sub):
            copy = send(own, c, "sub", s, sub, step, sub_send.at[step - 1, c], sub_recv.at[step - 1, c])
            copy.start()
            sent.append(copy)

    def product(slot, lower, count):
        depth = pl.ds(pl.multiple_of(slot * channels, channels), channels)
        return jnp.dot(
            gathered[slot, pl.ds(lower, count), :], weight[depth, :],
            preferred_element_type=jnp.float32,
        )

    load_weight.wait()
    total[...] = product(own, 0, tokens)
    for step in range(1, sub):
        slot = g * sub + lax.rem(s + sub - step, sub)
        for c in range(chunk_count):
            send(slot, c, "sub", s, sub, step, sub_send.at[step - 1, c], sub_recv.at[step - 1, c]).wait_recv()
        total[...] += product(slot, 0, tokens)

    def finish(c):
        lower = c * chunk
        for step in range(1, grp):
            source = lax.rem(g + grp - step, grp)
            for side in range(1, sub):
                slot = source * sub + lax.rem(s + sub - side, sub)
                sems = fwd_send.at[step - 1, side - 1, c], fwd_recv.at[step - 1, side - 1, c]
                send(slot, c, "sub", s, sub, side, *sems).wait_recv()
                total[pl.ds(lower, chunk), :] += product(slot, lower, chunk)
        out_ref[pl.ds(lower, chunk), :] = total[pl.ds(lower, chunk), :].astype(out_ref.dtype)

    for c in range(chunk_count):
        for step in range(1, grp):
            slot = lax.rem(g + grp - step, grp) * sub + s
            send(slot, c, "grp", g, grp, step, grp_send.at[step - 1, c], grp_recv.at[step - 1, c]).wait_recv()
            for side in range(1, sub):
                sems = fwd_send.at[step - 1, side - 1, c], fwd_recv.at[step - 1, side - 1, c]
                copy = send(slot, c, "sub", s, sub, side, *sems)
                copy.start()
                sent.append(copy)
            total[pl.ds(c * chunk, chunk), :] += product(slot, c * chunk, chunk)
        if c > 0:
            finish(c - 1)
    finish(chunk_count - 1)

    for copy in sent:
        copy.wait_send()
    pl.when(z < seq - 1)(send_halo.wait_send)
    for step in range(1, seq):
        pl.when(z + step < seq)(state_copies[step - 1].wait_send)


def shards(sizes, projected, short_filter, span_lengths, mode_rates, mode_residues, out_weight):
    seq, grp, sub, chunk_count = sizes
    tokens, _, channels = projected.shape
    modes = mode_rates.shape[0]
    pitch = -(-(channels // LANES) // 8) * 8
    mode_weight = mode_residues * jnp.sqrt(-jnp.expm1(-2.0 * mode_rates))
    packed = jnp.concatenate([mode_rates, mode_weight], axis=0)
    streams = projected.transpose(1, 0, 2)
    f32, bf16 = jnp.float32, jnp.bfloat16
    vmem = pl.BlockSpec(memory_space=pltpu.VMEM)
    dma = pltpu.SemaphoreType.DMA
    row_tile = pltpu.VMEM((tokens * pitch, LANES), f32)
    mask = pltpu.VMEM((tokens, LANES), f32)
    halo = pltpu.VMEM((6 * pitch, LANES), f32)
    state = (modes * pitch, LANES)
    return pl.pallas_call(
        functools.partial(kernel, sizes),
        out_shape=jax.ShapeDtypeStruct((tokens, out_weight.shape[1]), bf16),
        in_specs=[pl.BlockSpec(memory_space=pltpu.SMEM), vmem, vmem, vmem, pl.BlockSpec(memory_space=pl.ANY)],
        out_specs=vmem,
        scratch_shapes=[
            pltpu.VMEM(out_weight.shape, bf16),
            row_tile, row_tile, row_tile,
            pltpu.VMEM((9 * pitch, LANES), f32),
            pltpu.VMEM((2 * modes * pitch, LANES), f32),
            mask, mask, mask, halo, halo,
            pltpu.VMEM(state, f32),
            pltpu.VMEM((seq - 1,) + state, f32),
            pltpu.VMEM(state, f32),
            pltpu.VMEM((grp * sub, tokens, channels), bf16),
            pltpu.VMEM((tokens, out_weight.shape[1]), f32),
            dma, dma, dma,
            dma((seq - 1,)), dma((seq - 1,)),
            dma((sub - 1, chunk_count)), dma((sub - 1, chunk_count)),
            dma((grp - 1, chunk_count)), dma((grp - 1, chunk_count)),
            dma((grp - 1, sub - 1, chunk_count)), dma((grp - 1, sub - 1, chunk_count)),
        ],
        compiler_params=pltpu.CompilerParams(collective_id=0, has_side_effects=True),
    )(span_lengths, streams, short_filter, packed, out_weight)


def solution(mesh):
    sizes = (mesh.shape["seq"], mesh.shape["grp"], mesh.shape["sub"], 4)
    return jax.shard_map(
        functools.partial(shards, sizes),
        mesh=mesh,
        in_specs=(
            P(("parts", "seq"), None, ("grp", "sub")),
            P(None, None, ("grp", "sub")),
            P("parts"),
            P(None, ("grp", "sub")),
            P(None, ("grp", "sub")),
            P(None, ("grp", "sub")),
        ),
        out_specs=P(("parts", "seq"), ("grp", "sub")),
        check_vma=False,
    )
```

```python
import functools

import jax
import jax.numpy as jnp
from jax import lax
from jax.experimental import pallas as pl
from jax.experimental.pallas import tpu as pltpu
from jax.sharding import PartitionSpec as P

MESH = pl.DeviceIdType.MESH
LANES = 128


def tanh(x):
    x = jnp.clip(x, -7.90531110763549805, 7.90531110763549805)
    square = x * x
    top = jnp.full_like(x, -2.76076847742355e-16)
    for c in (
        2.00018790482477e-13, -8.60467152213735e-11, 5.12229709037114e-08,
        1.48572235717979e-05, 6.37261928875436e-04, 4.89352455891786e-03,
    ):
        top = top * square + c
    bottom = jnp.full_like(x, 1.19825839466702e-06)
    for c in (1.18534705686654e-04, 2.26843463243900e-03, 4.89352518554385e-03):
        bottom = bottom * square + c
    return jnp.where(jnp.abs(x) < 0.0004, x, x * top / bottom)


def kernel(
    sizes, spans_ref, x_ref, taps_ref, rates_ref, residues_ref, weight_hbm, out_ref,
    weight, xq, xk, xv, tap_rows, mode_rows, keep1, keep2, cont, final,
    gates, halo_out, halo_in, state_out, state_in, incoming, gathered, total,
    weight_sem, halo_send, halo_recv, state_send, state_recv,
    sub_send, sub_recv, grp_send, grp_recv, fwd_send, fwd_recv,
):
    seq, grp, sub, chunk_count = sizes
    _, tokens, channels = x_ref.shape
    modes, groups = rates_ref.shape
    rows = channels // LANES
    pitch = xq.shape[0] // tokens
    chunk = tokens // chunk_count
    z, g, s = lax.axis_index("seq"), lax.axis_index("grp"), lax.axis_index("sub")
    offset = z * tokens

    barrier = pltpu.get_barrier_semaphore()
    for axis, me, count in (("seq", z, seq), ("grp", g, grp), ("sub", s, sub)):
        for step in range(1, count):
            pl.semaphore_signal(
                barrier, inc=1, device_id={axis: lax.rem(me + step, count)}, device_id_type=MESH
            )
    load_weight = pltpu.make_async_copy(weight_hbm, weight, weight_sem)
    load_weight.start()

    if pitch != rows:
        for buffer in (xq, xk, xv, tap_rows, mode_rows):
            buffer[...] = jnp.zeros_like(buffer)
    for j, buffer in enumerate((xq, xk, xv)):
        for c in range(rows):
            lanes = slice(c * LANES, (c + 1) * LANES)
            buffer[pl.ds(c, tokens, stride=pitch), :] = x_ref[j, :, lanes].astype(jnp.float32)
    tail = 2 * pitch
    for j, buffer in enumerate((xq, xk, xv)):
        halo_out[pl.ds(j * tail, tail), :] = buffer[pl.ds(tokens * pitch - tail, tail), :]
    pl.semaphore_wait(barrier, seq + grp + sub - 3)

    send_halo = pltpu.make_async_remote_copy(
        src_ref=halo_out, dst_ref=halo_in, send_sem=halo_send, recv_sem=halo_recv,
        device_id={"seq": lax.rem(z + 1, seq)}, device_id_type=MESH,
    )

    @pl.when(z < seq - 1)
    def _():
        send_halo.start()

    tap_count = taps_ref.shape[0]
    for k in range(tap_count):
        for c in range(rows):
            for j in range(3):
                tap_rows[pl.ds((k * 3 + j) * pitch + c, 1), :] = taps_ref[
                    k, pl.ds(j, 1), c * LANES : (c + 1) * LANES
                ]
    group_size = channels // groups
    spread = (
        lax.broadcasted_iota(jnp.int32, (groups, channels), 1) // group_size
        == lax.broadcasted_iota(jnp.int32, (groups, channels), 0)
    ).astype(jnp.float32)
    rates = rates_ref[...]
    drop = tanh(rates) * (1.0 + jnp.exp(-2.0 * rates))
    for first, values in ((0, rates), (modes, residues_ref[...] * jnp.sqrt(drop))):
        wide = jnp.dot(
            values, spread, precision=lax.Precision.HIGHEST, preferred_element_type=jnp.float32
        )
        for c in range(rows):
            mode_rows[pl.ds(first * pitch + c, modes, stride=pitch), :] = wide[
                :, c * LANES : (c + 1) * LANES
            ]

    starts, start = [], jnp.int32(0)
    for i in range(spans_ref.shape[0]):
        starts.append(start)
        start = start + spans_ref[i]
    position = offset + lax.broadcasted_iota(jnp.int32, (tokens, LANES), 0)
    here = position == starts[0]
    before = position - 1 == starts[0]
    cut = (position >= starts[0]) & (starts[0] >= offset)
    ahead = (position < starts[0]) & (starts[0] < offset + tokens)
    for first in starts[1:]:
        here = here | (position == first)
        before = before | (position - 1 == first)
        cut = cut | ((position >= first) & (first >= offset))
        ahead = ahead | ((position < first) & (first < offset + tokens))
    keep1[...] = jnp.where(here, 0.0, 1.0)
    keep2[...] = jnp.where(here | before, 0.0, 1.0)
    cont[...] = jnp.where(cut, 0.0, 1.0)
    final[...] = jnp.where(ahead, 0.0, 1.0)

    def tile(ref, index):
        return ref[pl.ds(pl.multiple_of(index * pitch, pitch), pitch), :]

    rate = [tile(mode_rows, n) for n in range(modes)]
    decay = [jnp.exp(-rate[n]) for n in range(modes)]
    gain = [tile(mode_rows, modes + n) for n in range(modes)]
    taps = [[tile(tap_rows, k * 3 + j) for j in range(3)] for k in range(3)]

    unroll = 8

    def combine(parts):
        while len(parts) > 1:
            parts = [sum(parts[i + 1 : i + 2], parts[i]) for i in range(0, len(parts), 2)]
        return parts[0]

    def filtered(j, t, now, last, older):
        m1, m2 = keep1[pl.ds(t, 1), :], keep2[pl.ds(t, 1), :]
        return taps[0][j] * now + taps[1][j] * last * m1 + taps[2][j] * older * m2

    def gate(t, now, last, older):
        k, v = (filtered(j + 1, t, now[j], last[j], older[j]) for j in range(2))
        return (k * v).astype(jnp.bfloat16).astype(jnp.float32)

    def put(ref, t, value):
        ref[pl.ds(pl.multiple_of(t * pitch, pitch), pitch), :] = value

    def end_step(t, carry):
        last, older, state = carry
        now = [tile(buffer, t) for buffer in (xk, xv)]
        gated = gate(t, now, last, older)
        put(gates, t, gated)
        gated = gated * final[pl.ds(t, 1), :]
        return now, last, [decay[n] * state[n] + gated for n in range(modes)]

    def end_block(block, carry):
        for u in range(unroll):
            carry = end_step(block * unroll + u, carry)
        return carry

    first_rows = [[tile(buffer, t) for buffer in (xk, xv)] for t in range(2)]
    zero = [jnp.zeros((pitch, LANES), jnp.float32)] * modes
    carry = (first_rows[1], first_rows[0], zero)
    for t in range(2, unroll):
        carry = end_step(t, carry)
    _, _, state = lax.fori_loop(1, tokens // unroll, end_block, carry)

    @pl.when(z == 0)
    def _():
        halo_in[...] = jnp.zeros_like(halo_in)

    @pl.when(z > 0)
    def _():
        send_halo.wait_recv()

    older = [tile(halo_in, 2 * j) for j in (1, 2)]
    last = [tile(halo_in, 2 * j + 1) for j in (1, 2)]
    gated_0 = gate(0, first_rows[0], last, older)
    gated_1 = gate(1, first_rows[1], first_rows[0], last)
    put(gates, 0, gated_0)
    put(gates, 1, gated_1)
    gated_0, gated_1 = gated_0 * final[pl.ds(0, 1), :], gated_1 * final[pl.ds(1, 1), :]
    for n in range(modes):
        early = decay[n] * gated_0 + gated_1
        state_out[pl.ds(n * pitch, pitch), :] = state[n] + early * jnp.exp(
            -rate[n] * float(tokens - 2)
        )

    state_copies = []
    for step in range(1, seq):
        copy = pltpu.make_async_remote_copy(
            src_ref=state_out, dst_ref=state_in.at[step - 1],
            send_sem=state_send.at[step - 1], recv_sem=state_recv.at[step - 1],
            device_id={"seq": lax.rem(z + step, seq)}, device_id_type=MESH,
        )
        state_copies.append(copy)
        pl.when(z + step < seq)(copy.start)

    def own_block(block, carry):
        last, older, state = carry
        for u in range(unroll):
            t = block * unroll + u
            now, gated, m1 = tile(xq, t), tile(gates, t), keep1[pl.ds(t, 1), :]
            state = [decay[n] * (state[n] * m1) + gated for n in range(modes)]
            put(xk, t, combine([gain[n] * state[n] for n in range(modes)]))
            put(xq, t, filtered(0, t, now, last, older))
            last, older = now, last
        return last, older, state

    lax.fori_loop(0, tokens // unroll, own_block, (tile(halo_in, 1), tile(halo_in, 0), zero))
    incoming[...] = jnp.zeros_like(incoming)
    for step in range(1, seq):
        reach = (step - 1) * tokens
        open_ = jnp.float32(1.0)
        for first in starts:
            inside = (first >= offset - reach) & (first <= offset - 1)
            open_ = jnp.where(inside, 0.0, open_)

        @pl.when(z >= step)
        def _():
            state_copies[step - 1].wait_recv()
            for n in range(modes):
                at = pl.ds(n * pitch, pitch)
                factor = gain[n] * jnp.exp(-rate[n] * float(reach)) * open_
                incoming[at, :] += factor * state_in[step - 1, at, :]

    own = g * sub + s
    carried = [tile(incoming, n) for n in range(modes)]

    def correct_block(block, carry):
        for u in range(unroll):
            t = block * unroll + u
            carry = [decay[n] * carry[n] for n in range(modes)]
            came = combine(carry) * cont[pl.ds(t, 1), :]
            put(xv, t, tile(xq, t) * (tile(xk, t) + came))
        return carry

    def send(slot, c, axis, me, count, step, send_sem, recv_sem):
        piece = gathered.at[slot, pl.ds(c * chunk, chunk), :]
        return pltpu.make_async_remote_copy(
            src_ref=piece, dst_ref=piece, send_sem=send_sem, recv_sem=recv_sem,
            device_id={axis: lax.rem(me + step, count)}, device_id_type=MESH,
        )

    sent = []
    for c in range(chunk_count):
        per = chunk // unroll
        carried = lax.fori_loop(c * per, (c + 1) * per, correct_block, carried)
        for r in range(rows):
            gathered[own, pl.ds(c * chunk, chunk), r * LANES : (r + 1) * LANES] = xv[
                pl.ds(c * chunk * pitch + r, chunk, stride=pitch), :
            ].astype(jnp.bfloat16)
        for step in range(1, grp):
            copy = send(own, c, "grp", g, grp, step, grp_send.at[step - 1, c], grp_recv.at[step - 1, c])
            copy.start()
            sent.append(copy)
        for step in range(1, sub):
            copy = send(own, c, "sub", s, sub, step, sub_send.at[step - 1, c], sub_recv.at[step - 1, c])
            copy.start()
            sent.append(copy)

    def product(slot, lower, count):
        depth = pl.ds(pl.multiple_of(slot * channels, channels), channels)
        return jnp.dot(
            gathered[slot, pl.ds(lower, count), :], weight[depth, :],
            preferred_element_type=jnp.float32,
        )

    load_weight.wait()
    total[...] = product(own, 0, tokens)
    for step in range(1, sub):
        slot = g * sub + lax.rem(s + sub - step, sub)
        for c in range(chunk_count):
            send(slot, c, "sub", s, sub, step, sub_send.at[step - 1, c], sub_recv.at[step - 1, c]).wait_recv()
        total[...] += product(slot, 0, tokens)

    def finish(c):
        lower = c * chunk
        for step in range(1, grp):
            source = lax.rem(g + grp - step, grp)
            for side in range(1, sub):
                slot = source * sub + lax.rem(s + sub - side, sub)
                sems = fwd_send.at[step - 1, side - 1, c], fwd_recv.at[step - 1, side - 1, c]
                send(slot, c, "sub", s, sub, side, *sems).wait_recv()
                total[pl.ds(lower, chunk), :] += product(slot, lower, chunk)
        out_ref[pl.ds(lower, chunk), :] = total[pl.ds(lower, chunk), :].astype(out_ref.dtype)

    for c in range(chunk_count):
        for step in range(1, grp):
            slot = lax.rem(g + grp - step, grp) * sub + s
            send(slot, c, "grp", g, grp, step, grp_send.at[step - 1, c], grp_recv.at[step - 1, c]).wait_recv()
            for side in range(1, sub):
                sems = fwd_send.at[step - 1, side - 1, c], fwd_recv.at[step - 1, side - 1, c]
                copy = send(slot, c, "sub", s, sub, side, *sems)
                copy.start()
                sent.append(copy)
            total[pl.ds(c * chunk, chunk), :] += product(slot, c * chunk, chunk)
        if c > 0:
            finish(c - 1)
    finish(chunk_count - 1)

    for copy in sent:
        copy.wait_send()
    pl.when(z < seq - 1)(send_halo.wait_send)
    for step in range(1, seq):
        pl.when(z + step < seq)(state_copies[step - 1].wait_send)


def shards(sizes, projected, short_filter, span_lengths, mode_rates, mode_residues, out_weight):
    seq, grp, sub, chunk_count = sizes
    tokens, _, channels = projected.shape
    modes = mode_rates.shape[0]
    pitch = -(-(channels // LANES) // 8) * 8
    streams = projected.transpose(1, 0, 2)
    f32, bf16 = jnp.float32, jnp.bfloat16
    vmem = pl.BlockSpec(memory_space=pltpu.VMEM)
    dma = pltpu.SemaphoreType.DMA
    row_tile = pltpu.VMEM((tokens * pitch, LANES), f32)
    mask = pltpu.VMEM((tokens, LANES), f32)
    halo = pltpu.VMEM((6 * pitch, LANES), f32)
    state = (modes * pitch, LANES)
    return pl.pallas_call(
        functools.partial(kernel, sizes),
        out_shape=pltpu.VMEM((tokens, out_weight.shape[1]), bf16),
        in_specs=[pl.BlockSpec(memory_space=pltpu.SMEM), vmem, vmem, vmem, vmem, pl.BlockSpec(memory_space=pl.ANY)],
        out_specs=vmem,
        scratch_shapes=[
            pltpu.VMEM(out_weight.shape, bf16),
            row_tile, row_tile, row_tile,
            pltpu.VMEM((9 * pitch, LANES), f32),
            pltpu.VMEM((2 * modes * pitch, LANES), f32),
            mask, mask, mask, mask, row_tile, halo, halo,
            pltpu.VMEM(state, f32),
            pltpu.VMEM((seq - 1,) + state, f32),
            pltpu.VMEM(state, f32),
            pltpu.VMEM((grp * sub, tokens, channels), bf16),
            pltpu.VMEM((tokens, out_weight.shape[1]), f32),
            dma, dma, dma,
            dma((seq - 1,)), dma((seq - 1,)),
            dma((sub - 1, chunk_count)), dma((sub - 1, chunk_count)),
            dma((grp - 1, chunk_count)), dma((grp - 1, chunk_count)),
            dma((grp - 1, sub - 1, chunk_count)), dma((grp - 1, sub - 1, chunk_count)),
        ],
        compiler_params=pltpu.CompilerParams(collective_id=0, has_side_effects=True),
    )(span_lengths, streams, short_filter, mode_rates, mode_residues, out_weight)


def solution(mesh):
    sizes = (mesh.shape["seq"], mesh.shape["grp"], mesh.shape["sub"], 4)
    return jax.shard_map(
        functools.partial(shards, sizes),
        mesh=mesh,
        in_specs=(
            P(("parts", "seq"), None, ("grp", "sub")),
            P(None, None, ("grp", "sub")),
            P("parts"),
            P(None, ("grp", "sub")),
            P(None, ("grp", "sub")),
            P(None, ("grp", "sub")),
        ),
        out_specs=P(("parts", "seq"), ("grp", "sub")),
        check_vma=False,
    )
```

```python
import functools

import jax
import jax.numpy as jnp
from jax import lax
from jax.experimental import pallas as pl
from jax.experimental.pallas import tpu as pltpu
from jax.sharding import PartitionSpec as P

MESH = pl.DeviceIdType.MESH
LANES = 128


def tanh(x):
    x = jnp.clip(x, -7.90531110763549805, 7.90531110763549805)
    square = x * x
    top = jnp.full_like(x, -2.76076847742355e-16)
    for c in (
        2.00018790482477e-13, -8.60467152213735e-11, 5.12229709037114e-08,
        1.48572235717979e-05, 6.37261928875436e-04, 4.89352455891786e-03,
    ):
        top = top * square + c
    bottom = jnp.full_like(x, 1.19825839466702e-06)
    for c in (1.18534705686654e-04, 2.26843463243900e-03, 4.89352518554385e-03):
        bottom = bottom * square + c
    return jnp.where(jnp.abs(x) < 0.0004, x, x * top / bottom)


def kernel(
    sizes, spans_ref, x_hbm, taps_hbm, rates_hbm, residues_hbm, weight_hbm, out_ref,
    x_ref, taps_ref, rates_ref, residues_ref,
    weight, xq, xk, xv, tap_rows, mode_rows, keep1, keep2, cont, final,
    gates, halo_out, halo_in, state_out, state_in, incoming, gathered, total,
    load_sems, weight_sem, halo_send, halo_recv, state_send, state_recv,
    sub_send, sub_recv, grp_send, grp_recv, fwd_send, fwd_recv,
):
    seq, grp, sub, chunk_count = sizes
    _, tokens, channels = x_ref.shape
    modes, groups = rates_ref.shape
    rows = channels // LANES
    pitch = xq.shape[0] // tokens
    chunk = tokens // chunk_count
    z, g, s = lax.axis_index("seq"), lax.axis_index("grp"), lax.axis_index("sub")
    offset = z * tokens

    loads = [
        pltpu.make_async_copy(source, target, load_sems.at[i])
        for i, (source, target) in enumerate(
            ((taps_hbm, taps_ref), (rates_hbm, rates_ref), (residues_hbm, residues_ref), (x_hbm, x_ref))
        )
    ]
    for load in loads:
        load.start()

    barrier = pltpu.get_barrier_semaphore()
    for axis, me, count in (("seq", z, seq), ("grp", g, grp), ("sub", s, sub)):
        for step in range(1, count):
            pl.semaphore_signal(
                barrier, inc=1, device_id={axis: lax.rem(me + step, count)}, device_id_type=MESH
            )
    load_weight = pltpu.make_async_copy(weight_hbm, weight, weight_sem)
    load_weight.start()

    starts, start = [], jnp.int32(0)
    for i in range(spans_ref.shape[0]):
        starts.append(start)
        start = start + spans_ref[i]
    position = offset + lax.broadcasted_iota(jnp.int32, (tokens, LANES), 0)
    here = position == starts[0]
    before = position - 1 == starts[0]
    cut = (position >= starts[0]) & (starts[0] >= offset)
    ahead = (position < starts[0]) & (starts[0] < offset + tokens)
    for first in starts[1:]:
        here = here | (position == first)
        before = before | (position - 1 == first)
        cut = cut | ((position >= first) & (first >= offset))
        ahead = ahead | ((position < first) & (first < offset + tokens))
    keep1[...] = jnp.where(here, 0.0, 1.0)
    keep2[...] = jnp.where(here | before, 0.0, 1.0)
    cont[...] = jnp.where(cut, 0.0, 1.0)
    final[...] = jnp.where(ahead, 0.0, 1.0)

    if pitch != rows:
        for buffer in (xq, xk, xv, tap_rows, mode_rows):
            buffer[...] = jnp.zeros_like(buffer)
    for load in loads[:3]:
        load.wait()
    tap_count = taps_ref.shape[0]
    for k in range(tap_count):
        for c in range(rows):
            for j in range(3):
                tap_rows[pl.ds((k * 3 + j) * pitch + c, 1), :] = taps_ref[
                    k, pl.ds(j, 1), c * LANES : (c + 1) * LANES
                ]
    group_size = channels // groups
    spread = (
        lax.broadcasted_iota(jnp.int32, (groups, channels), 1) // group_size
        == lax.broadcasted_iota(jnp.int32, (groups, channels), 0)
    ).astype(jnp.float32)
    rates = rates_ref[...]
    drop = tanh(rates) * (1.0 + jnp.exp(-2.0 * rates))
    for first, values in ((0, rates), (modes, residues_ref[...] * jnp.sqrt(drop))):
        wide = jnp.dot(
            values, spread, precision=lax.Precision.HIGHEST, preferred_element_type=jnp.float32
        )
        for c in range(rows):
            mode_rows[pl.ds(first * pitch + c, modes, stride=pitch), :] = wide[
                :, c * LANES : (c + 1) * LANES
            ]

    loads[3].wait()
    for j, buffer in enumerate((xq, xk, xv)):
        for c in range(rows):
            lanes = slice(c * LANES, (c + 1) * LANES)
            buffer[pl.ds(c, tokens, stride=pitch), :] = x_ref[j, :, lanes].astype(jnp.float32)
    tail = 2 * pitch
    for j, buffer in enumerate((xq, xk, xv)):
        halo_out[pl.ds(j * tail, tail), :] = buffer[pl.ds(tokens * pitch - tail, tail), :]
    pl.semaphore_wait(barrier, seq + grp + sub - 3)

    send_halo = pltpu.make_async_remote_copy(
        src_ref=halo_out, dst_ref=halo_in, send_sem=halo_send, recv_sem=halo_recv,
        device_id={"seq": lax.rem(z + 1, seq)}, device_id_type=MESH,
    )

    @pl.when(z < seq - 1)
    def _():
        send_halo.start()

    def tile(ref, index):
        return ref[pl.ds(pl.multiple_of(index * pitch, pitch), pitch), :]

    rate = [tile(mode_rows, n) for n in range(modes)]
    decay = [jnp.exp(-rate[n]) for n in range(modes)]
    gain = [tile(mode_rows, modes + n) for n in range(modes)]
    taps = [[tile(tap_rows, k * 3 + j) for j in range(3)] for k in range(3)]

    unroll = 8

    def combine(parts):
        while len(parts) > 1:
            parts = [sum(parts[i + 1 : i + 2], parts[i]) for i in range(0, len(parts), 2)]
        return parts[0]

    def filtered(j, t, now, last, older):
        m1, m2 = keep1[pl.ds(t, 1), :], keep2[pl.ds(t, 1), :]
        return taps[0][j] * now + taps[1][j] * last * m1 + taps[2][j] * older * m2

    def gate(t, now, last, older):
        k, v = (filtered(j + 1, t, now[j], last[j], older[j]) for j in range(2))
        return (k * v).astype(jnp.bfloat16).astype(jnp.float32)

    def put(ref, t, value):
        ref[pl.ds(pl.multiple_of(t * pitch, pitch), pitch), :] = value

    def end_step(t, carry):
        last, older, state = carry
        now = [tile(buffer, t) for buffer in (xk, xv)]
        gated = gate(t, now, last, older)
        put(gates, t, gated)
        gated = gated * final[pl.ds(t, 1), :]
        return now, last, [decay[n] * state[n] + gated for n in range(modes)]

    def end_block(block, carry):
        for u in range(unroll):
            carry = end_step(block * unroll + u, carry)
        return carry

    first_rows = [[tile(buffer, t) for buffer in (xk, xv)] for t in range(2)]
    zero = [jnp.zeros((pitch, LANES), jnp.float32)] * modes
    carry = (first_rows[1], first_rows[0], zero)
    for t in range(2, unroll):
        carry = end_step(t, carry)
    _, _, state = lax.fori_loop(1, tokens // unroll, end_block, carry)

    @pl.when(z == 0)
    def _():
        halo_in[...] = jnp.zeros_like(halo_in)

    @pl.when(z > 0)
    def _():
        send_halo.wait_recv()

    older = [tile(halo_in, 2 * j) for j in (1, 2)]
    last = [tile(halo_in, 2 * j + 1) for j in (1, 2)]
    gated_0 = gate(0, first_rows[0], last, older)
    gated_1 = gate(1, first_rows[1], first_rows[0], last)
    put(gates, 0, gated_0)
    put(gates, 1, gated_1)
    gated_0, gated_1 = gated_0 * final[pl.ds(0, 1), :], gated_1 * final[pl.ds(1, 1), :]
    for n in range(modes):
        early = decay[n] * gated_0 + gated_1
        state_out[pl.ds(n * pitch, pitch), :] = state[n] + early * jnp.exp(
            -rate[n] * float(tokens - 2)
        )

    state_copies = []
    for step in range(1, seq):
        copy = pltpu.make_async_remote_copy(
            src_ref=state_out, dst_ref=state_in.at[step - 1],
            send_sem=state_send.at[step - 1], recv_sem=state_recv.at[step - 1],
            device_id={"seq": lax.rem(z + step, seq)}, device_id_type=MESH,
        )
        state_copies.append(copy)
    for step in reversed(range(1, seq)):
        pl.when(z + step < seq)(state_copies[step - 1].start)

    def own_block(block, carry):
        last, older, state = carry
        for u in range(unroll):
            t = block * unroll + u
            now, gated, m1 = tile(xq, t), tile(gates, t), keep1[pl.ds(t, 1), :]
            state = [decay[n] * (state[n] * m1) + gated for n in range(modes)]
            put(xk, t, combine([gain[n] * state[n] for n in range(modes)]))
            put(xq, t, filtered(0, t, now, last, older))
            last, older = now, last
        return last, older, state

    lax.fori_loop(0, tokens // unroll, own_block, (tile(halo_in, 1), tile(halo_in, 0), zero))
    incoming[...] = jnp.zeros_like(incoming)
    for step in range(1, seq):
        reach = (step - 1) * tokens
        open_ = jnp.float32(1.0)
        for first in starts:
            inside = (first >= offset - reach) & (first <= offset - 1)
            open_ = jnp.where(inside, 0.0, open_)

        @pl.when(z >= step)
        def _():
            state_copies[step - 1].wait_recv()
            for n in range(modes):
                at = pl.ds(n * pitch, pitch)
                factor = gain[n] * jnp.exp(-rate[n] * float(reach)) * open_
                incoming[at, :] += factor * state_in[step - 1, at, :]

    own = g * sub + s
    carried = [tile(incoming, n) for n in range(modes)]

    def correct_block(block, carry):
        for u in range(unroll):
            t = block * unroll + u
            carry = [decay[n] * carry[n] for n in range(modes)]
            came = combine(carry) * cont[pl.ds(t, 1), :]
            put(xv, t, tile(xq, t) * (tile(xk, t) + came))
        return carry

    def send(slot, c, axis, me, count, step, send_sem, recv_sem):
        piece = gathered.at[slot, pl.ds(c * chunk, chunk), :]
        return pltpu.make_async_remote_copy(
            src_ref=piece, dst_ref=piece, send_sem=send_sem, recv_sem=recv_sem,
            device_id={axis: lax.rem(me + step, count)}, device_id_type=MESH,
        )

    sent = []
    for c in range(chunk_count):
        per = chunk // unroll
        carried = lax.fori_loop(c * per, (c + 1) * per, correct_block, carried)
        for r in range(rows):
            gathered[own, pl.ds(c * chunk, chunk), r * LANES : (r + 1) * LANES] = xv[
                pl.ds(c * chunk * pitch + r, chunk, stride=pitch), :
            ].astype(jnp.bfloat16)
        for step in range(1, grp):
            copy = send(own, c, "grp", g, grp, step, grp_send.at[step - 1, c], grp_recv.at[step - 1, c])
            copy.start()
            sent.append(copy)
        for step in range(1, sub):
            copy = send(own, c, "sub", s, sub, step, sub_send.at[step - 1, c], sub_recv.at[step - 1, c])
            copy.start()
            sent.append(copy)

    def product(slot, lower, count):
        depth = pl.ds(pl.multiple_of(slot * channels, channels), channels)
        return jnp.dot(
            gathered[slot, pl.ds(lower, count), :], weight[depth, :],
            preferred_element_type=jnp.float32,
        )

    load_weight.wait()
    total[...] = product(own, 0, tokens)
    for step in range(1, sub):
        slot = g * sub + lax.rem(s + sub - step, sub)
        for c in range(chunk_count):
            send(slot, c, "sub", s, sub, step, sub_send.at[step - 1, c], sub_recv.at[step - 1, c]).wait_recv()
        total[...] += product(slot, 0, tokens)

    def finish(c):
        lower = c * chunk
        for step in range(1, grp):
            source = lax.rem(g + grp - step, grp)
            for side in range(1, sub):
                slot = source * sub + lax.rem(s + sub - side, sub)
                sems = fwd_send.at[step - 1, side - 1, c], fwd_recv.at[step - 1, side - 1, c]
                send(slot, c, "sub", s, sub, side, *sems).wait_recv()
                total[pl.ds(lower, chunk), :] += product(slot, lower, chunk)
        out_ref[pl.ds(lower, chunk), :] = total[pl.ds(lower, chunk), :].astype(out_ref.dtype)

    for c in range(chunk_count):
        for step in range(1, grp):
            slot = lax.rem(g + grp - step, grp) * sub + s
            send(slot, c, "grp", g, grp, step, grp_send.at[step - 1, c], grp_recv.at[step - 1, c]).wait_recv()
            for side in range(1, sub):
                sems = fwd_send.at[step - 1, side - 1, c], fwd_recv.at[step - 1, side - 1, c]
                copy = send(slot, c, "sub", s, sub, side, *sems)
                copy.start()
                sent.append(copy)
            total[pl.ds(c * chunk, chunk), :] += product(slot, c * chunk, chunk)
        if c > 0:
            finish(c - 1)
    finish(chunk_count - 1)

    for copy in sent:
        copy.wait_send()
    pl.when(z < seq - 1)(send_halo.wait_send)
    for step in range(1, seq):
        pl.when(z + step < seq)(state_copies[step - 1].wait_send)


def shards(sizes, projected, short_filter, span_lengths, mode_rates, mode_residues, out_weight):
    seq, grp, sub, chunk_count = sizes
    tokens, _, channels = projected.shape
    modes = mode_rates.shape[0]
    pitch = -(-(channels // LANES) // 8) * 8
    streams = projected.transpose(1, 0, 2)
    f32, bf16 = jnp.float32, jnp.bfloat16
    vmem = pl.BlockSpec(memory_space=pltpu.VMEM)
    hbm = pl.BlockSpec(memory_space=pl.ANY)
    dma = pltpu.SemaphoreType.DMA
    row_tile = pltpu.VMEM((tokens * pitch, LANES), f32)
    mask = pltpu.VMEM((tokens, LANES), f32)
    halo = pltpu.VMEM((6 * pitch, LANES), f32)
    state = (modes * pitch, LANES)
    return pl.pallas_call(
        functools.partial(kernel, sizes),
        out_shape=pltpu.VMEM((tokens, out_weight.shape[1]), bf16),
        in_specs=[pl.BlockSpec(memory_space=pltpu.SMEM), hbm, hbm, hbm, hbm, hbm],
        out_specs=vmem,
        scratch_shapes=[
            pltpu.VMEM(streams.shape, bf16),
            pltpu.VMEM(short_filter.shape, f32),
            pltpu.VMEM(mode_rates.shape, f32),
            pltpu.VMEM(mode_residues.shape, f32),
            pltpu.VMEM(out_weight.shape, bf16),
            row_tile, row_tile, row_tile,
            pltpu.VMEM((9 * pitch, LANES), f32),
            pltpu.VMEM((2 * modes * pitch, LANES), f32),
            mask, mask, mask, mask, row_tile, halo, halo,
            pltpu.VMEM(state, f32),
            pltpu.VMEM((seq - 1,) + state, f32),
            pltpu.VMEM(state, f32),
            pltpu.VMEM((grp * sub, tokens, channels), bf16),
            pltpu.VMEM((tokens, out_weight.shape[1]), f32),
            dma((4,)), dma, dma, dma,
            dma((seq - 1,)), dma((seq - 1,)),
            dma((sub - 1, chunk_count)), dma((sub - 1, chunk_count)),
            dma((grp - 1, chunk_count)), dma((grp - 1, chunk_count)),
            dma((grp - 1, sub - 1, chunk_count)), dma((grp - 1, sub - 1, chunk_count)),
        ],
        compiler_params=pltpu.CompilerParams(collective_id=0, has_side_effects=True),
    )(span_lengths, streams, short_filter, mode_rates, mode_residues, out_weight)


def solution(mesh):
    sizes = (mesh.shape["seq"], mesh.shape["grp"], mesh.shape["sub"], 4)
    return jax.shard_map(
        functools.partial(shards, sizes),
        mesh=mesh,
        in_specs=(
            P(("parts", "seq"), None, ("grp", "sub")),
            P(None, None, ("grp", "sub")),
            P("parts"),
            P(None, ("grp", "sub")),
            P(None, ("grp", "sub")),
            P(None, ("grp", "sub")),
        ),
        out_specs=P(("parts", "seq"), ("grp", "sub")),
        check_vma=False,
    )
```

```python
import functools

import jax
import jax.numpy as jnp
from jax import lax
from jax.experimental import pallas as pl
from jax.experimental.pallas import tpu as pltpu
from jax.sharding import PartitionSpec as P

MESH = pl.DeviceIdType.MESH
LANES = 128


def tanh(x):
    x = jnp.clip(x, -7.90531110763549805, 7.90531110763549805)
    square = x * x
    top = jnp.full_like(x, -2.76076847742355e-16)
    for c in (
        2.00018790482477e-13, -8.60467152213735e-11, 5.12229709037114e-08,
        1.48572235717979e-05, 6.37261928875436e-04, 4.89352455891786e-03,
    ):
        top = top * square + c
    bottom = jnp.full_like(x, 1.19825839466702e-06)
    for c in (1.18534705686654e-04, 2.26843463243900e-03, 4.89352518554385e-03):
        bottom = bottom * square + c
    return jnp.where(jnp.abs(x) < 0.0004, x, x * top / bottom)


def kernel(
    sizes, spans_ref, x_hbm, taps_hbm, rates_hbm, residues_hbm, weight_hbm, out_ref,
    x_ref, taps_ref, rates_ref, residues_ref,
    weight, xq, xk, xv, tap_rows, mode_rows, keep1, keep2, cont, final,
    gates, halo_out, halo_in, state_out, state_in, incoming, gathered, total,
    load_sems, weight_sem, halo_send, halo_recv, state_send, state_recv,
    sub_send, sub_recv, grp_send, grp_recv, fwd_send, fwd_recv,
):
    seq, grp, sub, chunk_count = sizes
    _, tokens, channels = x_ref.shape
    modes, groups = rates_ref.shape
    rows = channels // LANES
    pitch = xq.shape[0] // tokens
    chunk = tokens // chunk_count
    z, g, s = lax.axis_index("seq"), lax.axis_index("grp"), lax.axis_index("sub")
    offset = z * tokens

    loads = [
        pltpu.make_async_copy(source, target, load_sems.at[i])
        for i, (source, target) in enumerate(
            ((taps_hbm, taps_ref), (rates_hbm, rates_ref), (residues_hbm, residues_ref), (x_hbm, x_ref))
        )
    ]
    for load in loads:
        load.start()

    barrier = pltpu.get_barrier_semaphore()
    for axis, me, count in (("seq", z, seq), ("grp", g, grp), ("sub", s, sub)):
        for step in range(1, count):
            pl.semaphore_signal(
                barrier, inc=1, device_id={axis: lax.rem(me + step, count)}, device_id_type=MESH
            )
    load_weight = pltpu.make_async_copy(weight_hbm, weight, weight_sem)
    load_weight.start()

    starts, start = [], jnp.int32(0)
    for i in range(spans_ref.shape[0]):
        starts.append(start)
        start = start + spans_ref[i]
    position = offset + lax.broadcasted_iota(jnp.int32, (tokens, LANES), 0)
    here = position == starts[0]
    before = position - 1 == starts[0]
    cut = (position >= starts[0]) & (starts[0] >= offset)
    ahead = (position < starts[0]) & (starts[0] < offset + tokens)
    for first in starts[1:]:
        here = here | (position == first)
        before = before | (position - 1 == first)
        cut = cut | ((position >= first) & (first >= offset))
        ahead = ahead | ((position < first) & (first < offset + tokens))
    keep1[...] = jnp.where(here, 0.0, 1.0)
    keep2[...] = jnp.where(here | before, 0.0, 1.0)
    cont[...] = jnp.where(cut, 0.0, 1.0)
    final[...] = jnp.where(ahead, 0.0, 1.0)

    if pitch != rows:
        for buffer in (xq, xk, xv, tap_rows, mode_rows):
            buffer[...] = jnp.zeros_like(buffer)
    for load in loads[:3]:
        load.wait()
    tap_count = taps_ref.shape[0]
    for k in range(tap_count):
        for c in range(rows):
            for j in range(3):
                tap_rows[pl.ds((k * 3 + j) * pitch + c, 1), :] = taps_ref[
                    k, pl.ds(j, 1), c * LANES : (c + 1) * LANES
                ]
    group_size = channels // groups
    spread = (
        lax.broadcasted_iota(jnp.int32, (groups, channels), 1) // group_size
        == lax.broadcasted_iota(jnp.int32, (groups, channels), 0)
    ).astype(jnp.float32)
    rates = rates_ref[...]
    drop = tanh(rates) * (1.0 + jnp.exp(-2.0 * rates))
    for first, values in ((0, rates), (modes, residues_ref[...] * jnp.sqrt(drop))):
        wide = jnp.dot(
            values, spread, precision=lax.Precision.HIGHEST, preferred_element_type=jnp.float32
        )
        for c in range(rows):
            mode_rows[pl.ds(first * pitch + c, modes, stride=pitch), :] = wide[
                :, c * LANES : (c + 1) * LANES
            ]

    loads[3].wait()
    def lay_out(j, buffer, lower, upper):
        for c in range(rows):
            lanes = slice(c * LANES, (c + 1) * LANES)
            to = pl.ds(lower * pitch + c, upper - lower, stride=pitch)
            buffer[to, :] = x_ref[j, lower:upper, lanes].astype(jnp.float32)

    lay_out(0, xq, tokens - 16, tokens)
    lay_out(1, xk, 0, tokens)
    lay_out(2, xv, 0, tokens)
    tail = 2 * pitch
    for j, buffer in enumerate((xq, xk, xv)):
        halo_out[pl.ds(j * tail, tail), :] = buffer[pl.ds(tokens * pitch - tail, tail), :]
    pl.semaphore_wait(barrier, seq + grp + sub - 3)

    send_halo = pltpu.make_async_remote_copy(
        src_ref=halo_out, dst_ref=halo_in, send_sem=halo_send, recv_sem=halo_recv,
        device_id={"seq": lax.rem(z + 1, seq)}, device_id_type=MESH,
    )

    @pl.when(z < seq - 1)
    def _():
        send_halo.start()

    def tile(ref, index):
        return ref[pl.ds(pl.multiple_of(index * pitch, pitch), pitch), :]

    rate = [tile(mode_rows, n) for n in range(modes)]
    decay = [jnp.exp(-rate[n]) for n in range(modes)]
    gain = [tile(mode_rows, modes + n) for n in range(modes)]
    taps = [[tile(tap_rows, k * 3 + j) for j in range(3)] for k in range(3)]

    unroll = 8

    def combine(parts):
        while len(parts) > 1:
            parts = [sum(parts[i + 1 : i + 2], parts[i]) for i in range(0, len(parts), 2)]
        return parts[0]

    def filtered(j, t, now, last, older):
        m1, m2 = keep1[pl.ds(t, 1), :], keep2[pl.ds(t, 1), :]
        return taps[0][j] * now + taps[1][j] * last * m1 + taps[2][j] * older * m2

    def gate(t, now, last, older):
        k, v = (filtered(j + 1, t, now[j], last[j], older[j]) for j in range(2))
        return (k * v).astype(jnp.bfloat16).astype(jnp.float32)

    def put(ref, t, value):
        ref[pl.ds(pl.multiple_of(t * pitch, pitch), pitch), :] = value

    def end_step(t, carry):
        last, older, state = carry
        now = [tile(buffer, t) for buffer in (xk, xv)]
        gated = gate(t, now, last, older)
        put(gates, t, gated)
        gated = gated * final[pl.ds(t, 1), :]
        return now, last, [decay[n] * state[n] + gated for n in range(modes)]

    def end_block(block, carry):
        for u in range(unroll):
            carry = end_step(block * unroll + u, carry)
        return carry

    first_rows = [[tile(buffer, t) for buffer in (xk, xv)] for t in range(2)]
    zero = [jnp.zeros((pitch, LANES), jnp.float32)] * modes
    carry = (first_rows[1], first_rows[0], zero)
    for t in range(2, unroll):
        carry = end_step(t, carry)
    _, _, state = lax.fori_loop(1, tokens // unroll, end_block, carry)

    @pl.when(z == 0)
    def _():
        halo_in[...] = jnp.zeros_like(halo_in)

    @pl.when(z > 0)
    def _():
        send_halo.wait_recv()

    older = [tile(halo_in, 2 * j) for j in (1, 2)]
    last = [tile(halo_in, 2 * j + 1) for j in (1, 2)]
    gated_0 = gate(0, first_rows[0], last, older)
    gated_1 = gate(1, first_rows[1], first_rows[0], last)
    put(gates, 0, gated_0)
    put(gates, 1, gated_1)
    gated_0, gated_1 = gated_0 * final[pl.ds(0, 1), :], gated_1 * final[pl.ds(1, 1), :]
    for n in range(modes):
        early = decay[n] * gated_0 + gated_1
        state_out[pl.ds(n * pitch, pitch), :] = state[n] + early * jnp.exp(
            -rate[n] * float(tokens - 2)
        )

    state_copies = []
    for step in range(1, seq):
        copy = pltpu.make_async_remote_copy(
            src_ref=state_out, dst_ref=state_in.at[step - 1],
            send_sem=state_send.at[step - 1], recv_sem=state_recv.at[step - 1],
            device_id={"seq": lax.rem(z + step, seq)}, device_id_type=MESH,
        )
        state_copies.append(copy)
    for step in reversed(range(1, seq)):
        pl.when(z + step < seq)(state_copies[step - 1].start)

    lay_out(0, xq, 0, tokens - 16)

    def own_block(block, carry):
        last, older, state = carry
        for u in range(unroll):
            t = block * unroll + u
            now, gated, m1 = tile(xq, t), tile(gates, t), keep1[pl.ds(t, 1), :]
            state = [decay[n] * (state[n] * m1) + gated for n in range(modes)]
            put(xk, t, combine([gain[n] * state[n] for n in range(modes)]))
            put(xq, t, filtered(0, t, now, last, older))
            last, older = now, last
        return last, older, state

    lax.fori_loop(0, tokens // unroll, own_block, (tile(halo_in, 1), tile(halo_in, 0), zero))
    incoming[...] = jnp.zeros_like(incoming)
    for step in range(1, seq):
        reach = (step - 1) * tokens
        open_ = jnp.float32(1.0)
        for first in starts:
            inside = (first >= offset - reach) & (first <= offset - 1)
            open_ = jnp.where(inside, 0.0, open_)

        @pl.when(z >= step)
        def _():
            state_copies[step - 1].wait_recv()
            for n in range(modes):
                at = pl.ds(n * pitch, pitch)
                factor = gain[n] * jnp.exp(-rate[n] * float(reach)) * open_
                incoming[at, :] += factor * state_in[step - 1, at, :]

    own = g * sub + s
    carried = [tile(incoming, n) for n in range(modes)]

    def correct_block(block, carry):
        for u in range(unroll):
            t = block * unroll + u
            carry = [decay[n] * carry[n] for n in range(modes)]
            came = combine(carry) * cont[pl.ds(t, 1), :]
            put(xv, t, tile(xq, t) * (tile(xk, t) + came))
        return carry

    def send(slot, c, axis, me, count, step, send_sem, recv_sem):
        piece = gathered.at[slot, pl.ds(c * chunk, chunk), :]
        return pltpu.make_async_remote_copy(
            src_ref=piece, dst_ref=piece, send_sem=send_sem, recv_sem=recv_sem,
            device_id={axis: lax.rem(me + step, count)}, device_id_type=MESH,
        )

    sent = []
    for c in range(chunk_count):
        per = chunk // unroll
        carried = lax.fori_loop(c * per, (c + 1) * per, correct_block, carried)
        for r in range(rows):
            gathered[own, pl.ds(c * chunk, chunk), r * LANES : (r + 1) * LANES] = xv[
                pl.ds(c * chunk * pitch + r, chunk, stride=pitch), :
            ].astype(jnp.bfloat16)
        for step in range(1, grp):
            copy = send(own, c, "grp", g, grp, step, grp_send.at[step - 1, c], grp_recv.at[step - 1, c])
            copy.start()
            sent.append(copy)
        for step in range(1, sub):
            copy = send(own, c, "sub", s, sub, step, sub_send.at[step - 1, c], sub_recv.at[step - 1, c])
            copy.start()
            sent.append(copy)

    def product(slot, lower, count):
        depth = pl.ds(pl.multiple_of(slot * channels, channels), channels)
        return jnp.dot(
            gathered[slot, pl.ds(lower, count), :], weight[depth, :],
            preferred_element_type=jnp.float32,
        )

    load_weight.wait()
    total[...] = product(own, 0, tokens)
    for step in range(1, sub):
        slot = g * sub + lax.rem(s + sub - step, sub)
        for c in range(chunk_count):
            send(slot, c, "sub", s, sub, step, sub_send.at[step - 1, c], sub_recv.at[step - 1, c]).wait_recv()
        total[...] += product(slot, 0, tokens)

    def finish(c):
        lower = c * chunk
        for step in range(1, grp):
            source = lax.rem(g + grp - step, grp)
            for side in range(1, sub):
                slot = source * sub + lax.rem(s + sub - side, sub)
                sems = fwd_send.at[step - 1, side - 1, c], fwd_recv.at[step - 1, side - 1, c]
                send(slot, c, "sub", s, sub, side, *sems).wait_recv()
                total[pl.ds(lower, chunk), :] += product(slot, lower, chunk)
        out_ref[pl.ds(lower, chunk), :] = total[pl.ds(lower, chunk), :].astype(out_ref.dtype)

    for c in range(chunk_count):
        for step in range(1, grp):
            slot = lax.rem(g + grp - step, grp) * sub + s
            send(slot, c, "grp", g, grp, step, grp_send.at[step - 1, c], grp_recv.at[step - 1, c]).wait_recv()
            for side in range(1, sub):
                sems = fwd_send.at[step - 1, side - 1, c], fwd_recv.at[step - 1, side - 1, c]
                copy = send(slot, c, "sub", s, sub, side, *sems)
                copy.start()
                sent.append(copy)
            total[pl.ds(c * chunk, chunk), :] += product(slot, c * chunk, chunk)
        finish(c)

    for copy in sent:
        copy.wait_send()
    pl.when(z < seq - 1)(send_halo.wait_send)
    for step in range(1, seq):
        pl.when(z + step < seq)(state_copies[step - 1].wait_send)


def shards(sizes, projected, short_filter, span_lengths, mode_rates, mode_residues, out_weight):
    seq, grp, sub, chunk_count = sizes
    tokens, _, channels = projected.shape
    modes = mode_rates.shape[0]
    pitch = -(-(channels // LANES) // 8) * 8
    streams = projected.transpose(1, 0, 2)
    f32, bf16 = jnp.float32, jnp.bfloat16
    vmem = pl.BlockSpec(memory_space=pltpu.VMEM)
    hbm = pl.BlockSpec(memory_space=pl.ANY)
    dma = pltpu.SemaphoreType.DMA
    row_tile = pltpu.VMEM((tokens * pitch, LANES), f32)
    mask = pltpu.VMEM((tokens, LANES), f32)
    halo = pltpu.VMEM((6 * pitch, LANES), f32)
    state = (modes * pitch, LANES)
    return pl.pallas_call(
        functools.partial(kernel, sizes),
        out_shape=pltpu.VMEM((tokens, out_weight.shape[1]), bf16),
        in_specs=[pl.BlockSpec(memory_space=pltpu.SMEM), hbm, hbm, hbm, hbm, hbm],
        out_specs=vmem,
        scratch_shapes=[
            pltpu.VMEM(streams.shape, bf16),
            pltpu.VMEM(short_filter.shape, f32),
            pltpu.VMEM(mode_rates.shape, f32),
            pltpu.VMEM(mode_residues.shape, f32),
            pltpu.VMEM(out_weight.shape, bf16),
            row_tile, row_tile, row_tile,
            pltpu.VMEM((9 * pitch, LANES), f32),
            pltpu.VMEM((2 * modes * pitch, LANES), f32),
            mask, mask, mask, mask, row_tile, halo, halo,
            pltpu.VMEM(state, f32),
            pltpu.VMEM((seq - 1,) + state, f32),
            pltpu.VMEM(state, f32),
            pltpu.VMEM((grp * sub, tokens, channels), bf16),
            pltpu.VMEM((tokens, out_weight.shape[1]), f32),
            dma((4,)), dma, dma, dma,
            dma((seq - 1,)), dma((seq - 1,)),
            dma((sub - 1, chunk_count)), dma((sub - 1, chunk_count)),
            dma((grp - 1, chunk_count)), dma((grp - 1, chunk_count)),
            dma((grp - 1, sub - 1, chunk_count)), dma((grp - 1, sub - 1, chunk_count)),
        ],
        compiler_params=pltpu.CompilerParams(collective_id=0, has_side_effects=True),
    )(span_lengths, streams, short_filter, mode_rates, mode_residues, out_weight)


def solution(mesh):
    sizes = (mesh.shape["seq"], mesh.shape["grp"], mesh.shape["sub"], 4)
    return jax.shard_map(
        functools.partial(shards, sizes),
        mesh=mesh,
        in_specs=(
            P(("parts", "seq"), None, ("grp", "sub")),
            P(None, None, ("grp", "sub")),
            P("parts"),
            P(None, ("grp", "sub")),
            P(None, ("grp", "sub")),
            P(None, ("grp", "sub")),
        ),
        out_specs=P(("parts", "seq"), ("grp", "sub")),
        check_vma=False,
    )
```
